32 devices in a mesh: groups: 2 (over x), mesh: 16 (over z, y, core).
Axes of the slice: x: 2, y: 2, z: 4, core: 2. Of those that a mesh axis runs over, the one named last changes fastest.
Arguments:
- grid_in: bfloat16 [16384, 474], P(('groups', 'mesh')), parts along dimension 0, may hold values from -6 to 6
- owner: int32 [8192, 1], P('mesh'), may hold values from 0 to 15; in each aligned block of 512 rows (0 to 511, 512 to 1023, ...) at most 64 rows name the same one
- node_slot: int32 [8192], P('mesh'), may hold values from 0 to 255
- mesh_embed: bfloat16 [8192, 512], P(('groups', 'mesh')), parts along dimension 0, may hold values from -6 to 6
- edge_latent: bfloat16 [65536, 512], P(('groups', 'mesh')), parts along dimension 0, may hold values from -6 to 6
- senders: int32 [32768], P('mesh'), may hold values from 0 to 767
- receivers: int32 [32768], P('mesh'), may hold values from 0 to 255
- send_list: int32 [256, 32], P('mesh'), may hold values from 0 to 255
- w_grid_first: bfloat16 [474, 512], replicated, may hold values from -0.25 to 0.25
- w_grid_second: bfloat16 [512, 512], replicated, may hold values from -0.25 to 0.25
- w_enc_first: bfloat16 [1024, 512], replicated, may hold values from -0.1875 to 0.1875
- w_enc_second: bfloat16 [512, 512], replicated, may hold values from -0.25 to 0.25
- w_send: bfloat16 [512, 512], replicated, may hold values from -0.15625 to 0.15625
- w_recv: bfloat16 [512, 512], replicated, may hold values from -0.15625 to 0.15625
- w_edge: bfloat16 [512, 512], replicated, may hold values from -0.15625 to 0.15625
- w_message: bfloat16 [512, 512], replicated, may hold values from -0.25 to 0.25
- w_proc_first: bfloat16 [1024, 512], replicated, may hold values from -0.1875 to 0.1875
- w_proc_second: bfloat16 [512, 512], replicated, may hold values from -0.25 to 0.25
Outputs:
- mesh_out: bfloat16 [8192, 512], P(('groups', 'mesh')), parts along dimension 0
The draws below stay inside these ranges and needn't reach their ends.
There are 2 independent parts, one for each index of `groups`. The reference program is written for one: setup_inputs(seed, part) draws one part's arguments, and reference() takes and returns one part's arrays. A program takes and returns all parts, laid end to end along the dimension named above; an argument that names none is the same for every part. Nothing has to cross between parts.
Inputs may be any that keep to these rules, and one draw needn't show every extreme that they name: Among the grid points of one device at most 64 have the same owner, and some device has exactly 64 with one owner. Grid point g feeds node row node_slot[g] of device owner[g]. `senders`: A sender below 256 is a node row of the edge's own device; a sender 256 + p * 32 + j is row send_list[p * 16 + q, j] of device p, where q is the edge's device. `receivers`: edge k lies on device k // 2048; its receiver is a node row of that device. `send_list`: row p * 16 + q lists the 32 node rows of device p sent to device q.
All inputs are finite; a program needn't handle non-finite values.
Results may differ from the reference program's by a relative error of at most 0.0095.
Values may be sent and summed in bfloat16 or wider, within the bound.
A program may use at most 64 MiB of HBM per device.

```python
import math
import jax
import jax.numpy as jnp
import numpy as np
from jax import lax

D = 512
C_IN = 474
G_DEV = 512
NODE_DEV = 256
HALO_DEV = 512
CAP = 64
HCAP = 32
EDGE_DEV = 2048
GRID = 8192
NODES = 4096
EDGES = 32768
PAIRS = 256
N_MESH = 16


def plant(result, own_key, low, top_value):
    extent = result.shape
    place = [jax.random.randint(jax.random.fold_in(own_key, axis), (), 0, extent[axis]) for axis in range(len(extent))]
    result = result.at[tuple(place)].set(low)
    longest = extent.index(max(extent))
    place[longest] = (place[longest] + 1) % extent[longest]
    return result.at[tuple(place)].set(top_value)


def shard_levels(key, dims, pieces, smallest, largest):
    gain = 1.0
    for axis_at, blocks in pieces:
        steps = jax.random.uniform(jax.random.fold_in(jax.random.fold_in(key, 6), axis_at), (blocks,), jnp.float32, smallest / len(pieces), largest / len(pieces))
        gain = gain * jnp.repeat(jnp.exp(steps), dims[axis_at] // blocks).reshape((-1,) + (1,) * (len(dims) - 1 - axis_at))
    return gain


def deal_out(rng, own, number, rows, count, top, most, slope):
    order = jax.random.permutation(rng, count)
    crowded, usual = portions_of(count, rows * top, most, slope, True), portions_of(count, rows * top, most, slope, False)
    places = jnp.arange(count)

    def named(tallies, turn):
        used = int((tallies > 0).sum())
        fixed = max(1, used // 4)
        passed = fixed + (places - fixed + turn * (used - fixed)) % max(1, count - fixed)
        return jnp.zeros((count,), jnp.int32).at[order[jnp.where(places < fixed, places, passed)]].set(jnp.asarray(tallies, jnp.int32))

    tallies = jnp.where(number % 4 == 0, named(crowded, number // 4), named(usual, number - number // 4 - 1))
    mixed = jax.random.permutation(jax.random.fold_in(own, 3), count)
    source_of, receiver = mixed[0:count // 2 * 2:2], mixed[1:count // 2 * 2:2]
    room = jnp.minimum(tallies[source_of] - 1, most - tallies[receiver]) // 2
    room = jnp.where((source_of == order[0]) | (receiver == order[0]) | (tallies[receiver] == 0), 0, jnp.maximum(room, 0))
    passed = jax.random.randint(jax.random.fold_in(own, 4), (count // 2,), 0, 1 << 20) % (room + 1)
    tallies = tallies.at[source_of].add(-passed).at[receiver].add(passed)
    items = jnp.searchsorted(jnp.cumsum(tallies), jnp.arange(rows * top), side="right").astype(jnp.int32)
    grid = items.reshape(top, rows).T
    grid = grid[jax.random.permutation(jax.random.fold_in(own, 1), rows)]
    turn = jax.random.randint(jax.random.fold_in(own, 2), (rows, 1), 0, top)
    return jnp.take_along_axis(grid, (jnp.arange(top)[None, :] + turn) % top, axis=1)


def portions_of(count, total, limit, lean, full):
    weights = [(1 << 20) // math.isqrt(standing ** lean) + 1 for standing in range(1, count + 1)]
    largest = limit if full else min(limit, max(-(-total // count), total * weights[0] // sum(weights)))
    least = 1 if total - largest >= count - 1 else 0
    counts, surplus = [largest] + [least] * (count - 1), total - largest - least * (count - 1)
    while surplus > 0:
        movable = [i for i in range(1, count) if counts[i] < largest] or [i for i in range(1, count) if counts[i] < limit]
        whole, left = sum([weights[i] for i in movable]), surplus
        for i in movable:
            extra = min(limit - counts[i], max(1, left * weights[i] // whole), surplus)
            counts[i] = counts[i] + extra
            surplus = surplus - extra
    return np.array(counts)


def noise(key, shape, scale, limit, cuts=(), held_as=jnp.bfloat16):
    values = jax.random.normal(key, shape, jnp.float32) * scale
    if len(cuts) > 0:
        values = shard_levels(key, shape, cuts, -0.22, 0.18) * values
    return jnp.clip(values, min=-limit, max=limit).astype(held_as)


def setup_inputs(seed: int = 0, part: int = 0) -> dict:
    streams_of = jax.random.split(jax.random.key(seed), 19)
    own_keys = jax.random.split(jax.random.fold_in(streams_of[18], part), 19)
    grid_in = noise(own_keys[0], (GRID, C_IN), 1.0, 6.0, ((0, 16),))
    owner_keys = jax.random.split(jax.random.fold_in(streams_of[1], 1), GRID // G_DEV)
    owner_turns = jax.random.permutation(jax.random.fold_in(streams_of[1], 3), GRID // G_DEV)
    owner = jax.vmap(lambda own, number: deal_out(jax.random.fold_in(streams_of[1], 2), own, number, G_DEV, N_MESH, 1, CAP, 2))(owner_keys, owner_turns).reshape((GRID, 1))
    node_slot = plant(jax.random.randint(streams_of[2], (GRID,), 0, NODE_DEV), jax.random.fold_in(streams_of[2], 1), 0, NODE_DEV - 1).astype(jnp.int32)
    mesh_embed = noise(own_keys[3], (NODES, D), 1.0, 6.0, ((0, 16),))
    edge_latent = noise(own_keys[4], (EDGES, D), 1.0, 6.0, ((0, 16),))
    senders = plant(jax.random.randint(streams_of[5], (EDGES,), 0, NODE_DEV + HALO_DEV), jax.random.fold_in(streams_of[5], 1), 0, (NODE_DEV + HALO_DEV) - 1).astype(jnp.int32)
    receivers = plant(jax.random.randint(streams_of[6], (EDGES,), 0, NODE_DEV), jax.random.fold_in(streams_of[6], 1), 0, NODE_DEV - 1).astype(jnp.int32)
    send_list = plant(jax.random.randint(streams_of[7], (PAIRS, HCAP), 0, NODE_DEV), jax.random.fold_in(streams_of[7], 1), 0, NODE_DEV - 1).astype(jnp.int32)
    w_grid_first = noise(streams_of[8], (C_IN, D), C_IN ** -0.5, 0.25)
    w_grid_second = noise(streams_of[9], (D, D), D ** -0.5, 0.25)
    w_enc_first = noise(streams_of[10], (2 * D, D), (2 * D) ** -0.5, 0.1875)
    w_enc_second = noise(streams_of[11], (D, D), D ** -0.5, 0.25)
    w_send = noise(streams_of[12], (D, D), (3 * D) ** -0.5, 0.15625)
    w_recv = noise(streams_of[13], (D, D), (3 * D) ** -0.5, 0.15625)
    w_edge = noise(streams_of[14], (D, D), (3 * D) ** -0.5, 0.15625)
    w_message = noise(streams_of[15], (D, D), D ** -0.5, 0.25)
    w_proc_first = noise(streams_of[16], (2 * D, D), (2 * D) ** -0.5, 0.1875)
    w_proc_second = noise(streams_of[17], (D, D), D ** -0.5, 0.25)
    return dict(grid_in=grid_in, owner=owner, node_slot=node_slot, mesh_embed=mesh_embed, edge_latent=edge_latent, senders=senders, receivers=receivers, send_list=send_list, w_grid_first=w_grid_first, w_grid_second=w_grid_second, w_enc_first=w_enc_first, w_enc_second=w_enc_second, w_send=w_send, w_recv=w_recv, w_edge=w_edge, w_message=w_message, w_proc_first=w_proc_first, w_proc_second=w_proc_second)


def layer_norm(values):
    center = values - lax.optimization_barrier(jnp.mean(values, -1, keepdims=True))
    spread = lax.optimization_barrier(jnp.mean(center * center, -1, keepdims=True))
    return center * lax.rsqrt(spread + 1e-05)

def embed_grid(grid_rows, w_first, w_second):
    hidden = jax.nn.silu(jnp.dot(grid_rows, w_first, preferred_element_type=jnp.float32)).astype(jnp.bfloat16)
    return layer_norm(jnp.dot(hidden, w_second, preferred_element_type=jnp.float32)).astype(jnp.bfloat16)

def update_nodes(state, gathered, w_first, w_second):
    joined = jnp.concatenate([state.astype(jnp.float32), gathered], -1)
    normed = layer_norm(joined).astype(jnp.bfloat16)
    hidden = jax.nn.silu(jnp.dot(normed, w_first, preferred_element_type=jnp.float32)).astype(jnp.bfloat16)
    return (state.astype(jnp.float32) + jnp.dot(hidden, w_second, preferred_element_type=jnp.float32)).astype(jnp.bfloat16)

def reference(grid_in, owner, node_slot, mesh_embed, edge_latent, senders, receivers, send_list, w_grid_first, w_grid_second, w_enc_first, w_enc_second, w_send, w_recv, w_edge, w_message, w_proc_first, w_proc_second):
    grid_blocks = grid_in.reshape(N_MESH, G_DEV, C_IN)
    destination = (owner[:, 0] * NODE_DEV + node_slot).astype(jnp.int32).reshape(N_MESH, G_DEV)

    def add_grid(running, block):
        block_rows, block_dest = block
        latent = embed_grid(block_rows, w_grid_first, w_grid_second)
        return (running + jax.ops.segment_sum(latent.astype(jnp.float32), block_dest, num_segments=NODES), None)
    g2m_sum, _ = lax.scan(add_grid, jnp.zeros((NODES, D), jnp.float32), (grid_blocks, destination))
    mesh_latent = update_nodes(mesh_embed, g2m_sum, w_enc_first, w_enc_second)
    device_of = (jnp.arange(EDGES, dtype=jnp.int32) // EDGE_DEV).astype(jnp.int32)
    global_recv = (device_of * NODE_DEV + receivers).astype(jnp.int32)
    halo_pos = jnp.maximum(senders - NODE_DEV, 0).astype(jnp.int32)
    source_peer = (halo_pos // HCAP).astype(jnp.int32)
    source_slot = (halo_pos % HCAP).astype(jnp.int32)
    remote = source_peer * NODE_DEV + send_list[source_peer * N_MESH + device_of, source_slot]
    global_send = jnp.where(senders < NODE_DEV, device_of * NODE_DEV + senders, remote).astype(jnp.int32)
    edge_blocks = edge_latent.reshape(N_MESH, EDGE_DEV, D)
    send_blocks = global_send.reshape(N_MESH, EDGE_DEV)
    recv_blocks = global_recv.reshape(N_MESH, EDGE_DEV)

    def add_edges(running, block):
        block_edges, block_send, block_recv = block
        pre = jnp.dot(mesh_latent[block_send], w_send, preferred_element_type=jnp.float32)
        pre = pre + jnp.dot(mesh_latent[block_recv], w_recv, preferred_element_type=jnp.float32)
        pre = pre + jnp.dot(block_edges, w_edge, preferred_element_type=jnp.float32)
        hidden = jax.nn.silu(pre).astype(jnp.bfloat16)
        message = jnp.dot(hidden, w_message, preferred_element_type=jnp.float32)
        return (running + jax.ops.segment_sum(message, block_recv, num_segments=NODES), None)
    node_sum, _ = lax.scan(add_edges, jnp.zeros((NODES, D), jnp.float32), (edge_blocks, send_blocks, recv_blocks))
    return update_nodes(mesh_latent, node_sum, w_proc_first, w_proc_second)
```

```python
import functools

import jax
import jax.numpy as jnp
from jax import lax
from jax.experimental import pallas as pl
from jax.experimental.pallas import tpu as pltpu
from jax.sharding import PartitionSpec as P

F32 = jnp.float32
BF16 = jnp.bfloat16
MESH = pl.DeviceIdType.MESH
GROUP = 256
CHUNK = 256
LANES = 128


def dot(left, right):
    return jnp.dot(left, right, preferred_element_type=F32)


def silu(x):
    half = 0.5 * x
    return half * jnp.tanh(half) + half


def normalize(values):
    center = values - jnp.mean(values, -1, keepdims=True)
    spread = jnp.mean(center * center, -1, keepdims=True)
    return center * lax.rsqrt(spread + 1e-05)


def hot(flags):
    return jnp.where(flags, 1.0, 0.0).astype(BF16)


def update(state, gathered, w_first, w_second):
    width = state.shape[1]
    rows = state.astype(F32)
    mean = (
        jnp.sum(rows, -1, keepdims=True) + jnp.sum(gathered, -1, keepdims=True)
    ) / (2 * width)
    low, high = rows - mean, gathered - mean
    spread = (
        jnp.sum(low * low, -1, keepdims=True) + jnp.sum(high * high, -1, keepdims=True)
    ) / (2 * width)
    scale = lax.rsqrt(spread + 1e-05)
    hidden = dot((low * scale).astype(BF16), w_first[:width, :])
    hidden = hidden + dot((high * scale).astype(BF16), w_first[width:, :])
    return (rows + dot(silu(hidden).astype(BF16), w_second[...])).astype(BF16)


def kernel(n, cap, hcap, *refs):
    hbm = refs[:18]
    out_ref = refs[18]
    (
        grid_in,
        owner,
        node_slot,
        embed,
        edges,
        senders,
        receivers,
        send_list,
        w_grid_first,
        w_grid_second,
        w_enc_first,
        w_enc_second,
        w_send,
        w_recv,
        w_edge,
        w_message,
        w_proc_first,
        w_proc_second,
    ) = vmem = refs[19:37]
    (
        latent,
        outgoing,
        arrived,
        ids_out,
        ids_in,
        pre,
        local_table,
        near_hot,
        halo_hot,
        node_hot,
        list_hot,
        halo_out,
        halo_in,
        load_sem,
        row_send,
        row_recv,
        id_send,
        id_recv,
        halo_send,
        halo_recv,
    ) = refs[37:]
    grid_count = grid_in.shape[0]
    nodes, width = embed.shape
    edge_count = edges.shape[0]
    me = lax.axis_index("mesh")

    def offset(t):
        return n // 2 - (t + 1) // 2 if t % 2 else n // 2 + t // 2

    def peer(t):
        return lax.rem(me + offset(t), n)

    loads = [
        pltpu.make_async_copy(source, target, load_sem.at[i])
        for i, (source, target) in enumerate(zip(hbm, vmem))
    ]
    for i in (0, 8, 1, 2, 9, 14, 4, 3, 10, 11, 7, 12, 13, 5, 6, 15, 16, 17):
        loads[i].start()
    barrier = pltpu.get_barrier_semaphore()
    for t in range(n - 1):
        pl.semaphore_signal(barrier, inc=1, device_id={"mesh": peer(t)}, device_id_type=MESH)

    loads[1].wait()
    loads[2].wait()
    step = lax.broadcasted_iota(jnp.int32, (n, 1), 0)
    turn = n // 2 + jnp.where(step % 2 == 1, -((step + 1) // 2), step // 2)
    target = lax.rem(me + turn, n)
    flags = jnp.where(target == owner[...], 1.0, 0.0)
    earlier = hot(
        lax.broadcasted_iota(jnp.int32, (grid_count, grid_count), 0)
        < lax.broadcasted_iota(jnp.int32, (grid_count, grid_count), 1)
    )
    rank = dot(flags.astype(BF16), earlier) + (step * cap).astype(F32)
    place = jnp.sum(flags * rank, 0, keepdims=True).astype(jnp.int32)
    slots = (flags * (node_slot[...] + 1).astype(F32)).astype(BF16)
    lane_hot = hot(
        lax.broadcasted_iota(jnp.int32, (GROUP, grid_count), 0) == place % GROUP
    )
    ids = lax.dot_general(slots, lane_hot, (((1,), (1,)), ((), ())), preferred_element_type=F32)
    for t in range(n):
        ids_out[t] = ids[t : t + 1, :]
    ids_in[n - 1] = ids[n - 1 : n, :]

    loads[0].wait()
    loads[8].wait()
    loads[9].wait()
    hidden = silu(dot(grid_in[...], w_grid_first[...])).astype(BF16)
    latent[...] = normalize(dot(hidden, w_grid_second[...])).astype(BF16)

    pl.semaphore_wait(barrier, n - 1)
    per_group = GROUP // cap
    copies = []
    for group in range(n // per_group):
        pack = hot(
            lax.broadcasted_iota(jnp.int32, (GROUP, grid_count), 0) + group * GROUP == place
        )
        block = dot(pack, latent[...]).astype(BF16)
        first = group * per_group
        outgoing[first : first + per_group] = block.reshape(per_group, cap, width)
        for t in range(first, min(first + per_group, n - 1)):
            id_copy = pltpu.make_async_remote_copy(
                src_ref=ids_out.at[t],
                dst_ref=ids_in.at[t],
                send_sem=id_send.at[t],
                recv_sem=id_recv.at[t],
                device_id={"mesh": peer(t)},
                device_id_type=MESH,
            )
            row_copy = pltpu.make_async_remote_copy(
                src_ref=outgoing.at[t],
                dst_ref=arrived.at[t],
                send_sem=row_send.at[t],
                recv_sem=row_recv.at[t],
                device_id={"mesh": peer(t)},
                device_id_type=MESH,
            )
            id_copy.start()
            row_copy.start()
            copies.append((id_copy, row_copy))
    arrived[n - 1] = outgoing[n - 1]

    loads[14].wait()
    loads[4].wait()
    for chunk in range(edge_count // CHUNK):
        rows = pl.ds(chunk * CHUNK, CHUNK)
        pre[rows, :] = dot(edges[rows, :], w_edge[...])
    loads[5].wait()
    loads[6].wait()
    loads[7].wait()
    sender_columns = jnp.transpose(senders[...])
    receiver_columns = jnp.transpose(receivers[...])
    list_columns = jnp.transpose(send_list[...])
    near_iota = lax.broadcasted_iota(jnp.int32, (LANES, nodes), 1)
    halo_iota = lax.broadcasted_iota(jnp.int32, (LANES, n * hcap), 1) + nodes
    node_iota = lax.broadcasted_iota(jnp.int32, (nodes, LANES), 0)
    for part in range(edge_count // LANES):
        rows = pl.ds(part * LANES, LANES)
        sender = sender_columns[:, part : part + 1]
        receiver = receiver_columns[:, part : part + 1]
        near_hot[rows, :nodes] = hot(sender == near_iota)
        near_hot[rows, nodes:] = hot(receiver == near_iota)
        halo_hot[rows, :] = hot(sender == halo_iota)
        node_hot[:, part * LANES : (part + 1) * LANES] = hot(
            receivers[part : part + 1, :] == node_iota
        )
    list_iota = lax.broadcasted_iota(jnp.int32, (hcap, nodes), 1)
    for p in range(n):
        list_hot[p * hcap : (p + 1) * hcap, :] = hot(list_columns[:, p : p + 1] == list_iota)

    gathered = jnp.zeros((nodes, width), F32)
    slot_iota = lax.broadcasted_iota(jnp.int32, (nodes, GROUP), 0).astype(F32) + 1.0
    for group in range(n // per_group):
        first = group * per_group
        named = jnp.zeros((1, GROUP), F32)
        for t in range(first, first + per_group):
            if t < n - 1:
                copies[t][0].wait_recv()
                copies[t][1].wait_recv()
            named = named + ids_in[t]
        gathered = gathered + dot(
            hot(slot_iota == named),
            arrived[first : first + per_group].reshape(GROUP, width),
        )

    for i in (3, 10, 11, 12, 13):
        loads[i].wait()
    state = update(embed[...], gathered, w_enc_first, w_enc_second)
    sent = dot(state, w_send[...]).astype(BF16)
    halo_out[...] = dot(list_hot[...], sent).astype(BF16).reshape(n, hcap, width)
    halo_copies = []
    for t in range(n - 1):
        copy = pltpu.make_async_remote_copy(
            src_ref=halo_out.at[peer(t)],
            dst_ref=halo_in.at[me],
            send_sem=halo_send.at[t],
            recv_sem=halo_recv.at[t],
            device_id={"mesh": peer(t)},
            device_id_type=MESH,
        )
        copy.start()
        halo_copies.append(copy)
    halo_in[me] = halo_out[me]
    local_table[:nodes, :] = sent
    local_table[nodes:, :] = dot(state, w_recv[...]).astype(BF16)
    for chunk in range(edge_count // CHUNK):
        rows = pl.ds(chunk * CHUNK, CHUNK)
        pre[rows, :] += dot(near_hot[rows, :], local_table[...])

    for copy in halo_copies:
        copy.wait_recv()
    halo = halo_in[...].reshape(n * hcap, width)
    summed = jnp.zeros((nodes, width), F32)
    for chunk in range(edge_count // CHUNK):
        rows = pl.ds(chunk * CHUNK, CHUNK)
        edge_pre = pre[rows, :] + dot(halo_hot[rows, :], halo)
        summed = summed + dot(
            node_hot[:, chunk * CHUNK : (chunk + 1) * CHUNK], silu(edge_pre).astype(BF16)
        )
    for i in (15, 16, 17):
        loads[i].wait()
    node_sum = dot(summed.astype(BF16), w_message[...])
    out_ref[...] = update(state, node_sum, w_proc_first, w_proc_second)
    for id_copy, row_copy in copies:
        id_copy.wait_send()
        row_copy.wait_send()
    for copy in halo_copies:
        copy.wait_send()


def per_device(
    grid_in, owner, node_slot, mesh_embed, edge_latent, senders, receivers, send_list, *weights
):
    n = lax.axis_size("mesh")
    grid_count = grid_in.shape[0]
    nodes, width = mesh_embed.shape
    edge_count = edge_latent.shape[0]
    list_size = send_list.shape[1]
    cap = max(16, 2 * grid_count // n)
    hcap = max(16, list_size)
    if hcap != list_size:
        beyond = jnp.maximum(senders - nodes, 0)
        moved = nodes + beyond // list_size * hcap + beyond % list_size
        senders = jnp.where(senders < nodes, senders, moved)
        send_list = jnp.pad(send_list, ((0, 0), (0, hcap - list_size)))
    inputs = (
        grid_in,
        owner.reshape(1, grid_count),
        node_slot.reshape(1, grid_count),
        mesh_embed,
        edge_latent,
        senders.reshape(edge_count // LANES, LANES),
        receivers.reshape(edge_count // LANES, LANES),
        send_list,
    ) + weights
    dma = pltpu.SemaphoreType.DMA
    scratch = [pltpu.VMEM(x.shape, x.dtype) for x in inputs] + [
        pltpu.VMEM((grid_count, width), BF16),
        pltpu.VMEM((n, cap, width), BF16),
        pltpu.VMEM((n, cap, width), BF16),
        pltpu.VMEM((n, 1, GROUP), F32),
        pltpu.VMEM((n, 1, GROUP), F32),
        pltpu.VMEM((edge_count, width), F32),
        pltpu.VMEM((2 * nodes, width), BF16),
        pltpu.VMEM((edge_count, 2 * nodes), BF16),
        pltpu.VMEM((edge_count, n * hcap), BF16),
        pltpu.VMEM((nodes, edge_count), BF16),
        pltpu.VMEM((n * hcap, nodes), BF16),
        pltpu.VMEM((n, hcap, width), BF16),
        pltpu.VMEM((n, hcap, width), BF16),
        dma((len(inputs),)),
        dma((n,)),
        dma((n,)),
        dma((n,)),
        dma((n,)),
        dma((n,)),
        dma((n,)),
    ]
    return pl.pallas_call(
        functools.partial(kernel, n, cap, hcap),
        out_shape=jax.ShapeDtypeStruct((nodes, width), BF16),
        in_specs=[pl.BlockSpec(memory_space=pl.ANY)] * len(inputs),
        out_specs=pl.BlockSpec(memory_space=pltpu.VMEM),
        scratch_shapes=scratch,
        compiler_params=pltpu.CompilerParams(
            collective_id=0, has_side_effects=True, vmem_limit_bytes=56 << 20
        ),
    )(*inputs)


def solution(mesh):
    rows, split, full = P(("groups", "mesh"), None), P("mesh"), P()
    in_specs = (rows, split, split, rows, rows, split, split, split) + (full,) * 10
    return jax.shard_map(
        per_device, mesh=mesh, in_specs=in_specs, out_specs=rows, check_vma=False
    )
```

```python
import functools

import jax
import jax.numpy as jnp
from jax import lax
from jax.experimental import pallas as pl
from jax.experimental.pallas import tpu as pltpu
from jax.sharding import PartitionSpec as P

F32 = jnp.float32
BF16 = jnp.bfloat16
MESH = pl.DeviceIdType.MESH
GROUP = 256
CHUNK = 256
LANES = 128


def dot(left, right):
    return jnp.dot(left, right, preferred_element_type=F32)


def silu(x):
    half = 0.5 * x
    return half * jnp.tanh(half) + half


def normalize(values):
    center = values - jnp.mean(values, -1, keepdims=True)
    spread = jnp.mean(center * center, -1, keepdims=True)
    return center * lax.rsqrt(spread + 1e-05)


def hot(flags):
    return jnp.where(flags, 1.0, 0.0).astype(BF16)


def update(state, gathered, w_first, w_second):
    width = state.shape[1]
    rows = state.astype(F32)
    mean = (
        jnp.sum(rows, -1, keepdims=True) + jnp.sum(gathered, -1, keepdims=True)
    ) / (2 * width)
    low, high = rows - mean, gathered - mean
    spread = (
        jnp.sum(low * low, -1, keepdims=True) + jnp.sum(high * high, -1, keepdims=True)
    ) / (2 * width)
    scale = lax.rsqrt(spread + 1e-05)
    hidden = dot((low * scale).astype(BF16), w_first[:width, :])
    hidden = hidden + dot((high * scale).astype(BF16), w_first[width:, :])
    return (rows + dot(silu(hidden).astype(BF16), w_second[...])).astype(BF16)


def kernel(n, cap, hcap, *refs):
    hbm = refs[:18]
    out_ref = refs[18]
    (
        grid_in,
        owner,
        node_slot,
        embed,
        edges,
        senders,
        receivers,
        send_list,
        w_grid_first,
        w_grid_second,
        w_enc_first,
        w_enc_second,
        w_send,
        w_recv,
        w_edge,
        w_message,
        w_proc_first,
        w_proc_second,
    ) = vmem = refs[19:37]
    (
        latent,
        outgoing,
        arrived,
        ids_out,
        ids_in,
        pre,
        local_table,
        near_hot,
        halo_hot,
        node_hot,
        list_hot,
        halo_out,
        halo_in,
        relay_out,
        relay_in,
        relay_sem,
        load_sem,
        row_send,
        row_recv,
        id_send,
        id_recv,
        halo_send,
        halo_recv,
    ) = refs[37:]
    grid_count = grid_in.shape[1]
    nodes, width = embed.shape
    edge_count = edges.shape[0]
    me = lax.axis_index("mesh")

    half = n // 2
    base = me // half * half
    mirror = lax.rem(me + half, n)

    def around(t, count):
        return count // 2 - (t + 1) // 2 if t % 2 else count // 2 + t // 2

    def peer(t):
        return lax.rem(me + around(t, n), n)

    def near_peer(t):
        return base + lax.rem(me + around(t, half), half)

    loads = [
        pltpu.make_async_copy(source, target, load_sem.at[i])
        for i, (source, target) in enumerate(zip(hbm, vmem))
    ]
    for i in (0, 8, 1, 2, 9, 14, 4, 3, 10, 11, 7, 12, 13, 5, 6, 15, 16, 17):
        loads[i].start()
    barrier = pltpu.get_barrier_semaphore()
    for t in range(n - 1):
        pl.semaphore_signal(barrier, inc=1, device_id={"mesh": peer(t)}, device_id_type=MESH)

    loads[1].wait()
    loads[2].wait()
    block = lax.broadcasted_iota(jnp.int32, (n, 1), 0)
    step = lax.rem(block, half)
    turn = half // 2 + jnp.where(step % 2 == 1, -((step + 1) // 2), step // 2)
    target = base + lax.rem(me + turn, half)
    target = jnp.where(block < half, lax.rem(target + half, n), target)
    flags = jnp.where(target == owner[...], 1.0, 0.0)
    earlier = hot(
        lax.broadcasted_iota(jnp.int32, (grid_count, grid_count), 0)
        < lax.broadcasted_iota(jnp.int32, (grid_count, grid_count), 1)
    )
    rank = dot(flags.astype(BF16), earlier) + (block * cap).astype(F32)
    place = jnp.sum(flags * rank, 0, keepdims=True).astype(jnp.int32)
    slots = (flags * (node_slot[...] + 1).astype(F32)).astype(BF16)
    lane_hot = hot(
        lax.broadcasted_iota(jnp.int32, (GROUP, grid_count), 0) == place % GROUP
    )
    ids = lax.dot_general(slots, lane_hot, (((1,), (1,)), ((), ())), preferred_element_type=F32)
    for t in range(n):
        ids_out[t] = ids[t : t + 1, :]
    for t in (half - 1, n - 1):
        ids_in[t] = ids[t : t + 1, :]

    loads[0].wait()
    loads[8].wait()
    loads[9].wait()
    hidden = lax.dot_general(
        grid_in[...], w_grid_first[...], (((0,), (0,)), ((), ())), preferred_element_type=F32
    )
    hidden = silu(hidden).astype(BF16)
    latent[...] = normalize(dot(hidden, w_grid_second[...])).astype(BF16)

    pl.semaphore_wait(barrier, n - 1)
    per_group = GROUP // cap
    copies = {}
    for group in range(n // per_group):
        pack = hot(
            lax.broadcasted_iota(jnp.int32, (GROUP, grid_count), 0) + group * GROUP == place
        )
        packed = dot(pack, latent[...]).astype(BF16)
        first = group * per_group
        outgoing[first : first + per_group] = packed.reshape(per_group, cap, width)
        for t in range(first, first + per_group):
            if t % half == half - 1:
                arrived[t] = outgoing[t]
                continue
            id_copy = pltpu.make_async_remote_copy(
                src_ref=ids_out.at[t],
                dst_ref=ids_in.at[t],
                send_sem=id_send.at[t],
                recv_sem=id_recv.at[t],
                device_id={"mesh": near_peer(t % half)},
                device_id_type=MESH,
            )
            row_copy = pltpu.make_async_remote_copy(
                src_ref=outgoing.at[t],
                dst_ref=arrived.at[t],
                send_sem=row_send.at[t],
                recv_sem=row_recv.at[t],
                device_id={"mesh": near_peer(t % half)},
                device_id_type=MESH,
            )
            id_copy.start()
            row_copy.start()
            copies[t] = (id_copy, row_copy)

    loads[14].wait()
    loads[4].wait()
    for chunk in range(edge_count // CHUNK):
        rows = pl.ds(chunk * CHUNK, CHUNK)
        pre[rows, :] = dot(edges[rows, :], w_edge[...])

    slot_iota = lax.broadcasted_iota(jnp.int32, (nodes, GROUP), 0).astype(F32) + 1.0

    def collect(start, stop):
        total = jnp.zeros((nodes, width), F32)
        for first in range(start, stop, per_group):
            named = jnp.zeros((1, GROUP), F32)
            for t in range(first, first + per_group):
                if t in copies:
                    copies[t][0].wait_recv()
                    copies[t][1].wait_recv()
                named = named + ids_in[t]
            total = total + dot(
                hot(slot_iota == named),
                arrived[first : first + per_group].reshape(GROUP, width),
            )
        return total

    relay_out[...] = collect(0, half).astype(BF16)
    relay = pltpu.make_async_remote_copy(
        src_ref=relay_out,
        dst_ref=relay_in,
        send_sem=relay_sem.at[0],
        recv_sem=relay_sem.at[1],
        device_id={"mesh": mirror},
        device_id_type=MESH,
    )
    relay.start()

    loads[5].wait()
    loads[6].wait()
    loads[7].wait()
    sender_columns = jnp.transpose(senders[...])
    receiver_columns = jnp.transpose(receivers[...])
    list_columns = jnp.transpose(send_list[...])
    near_iota = lax.broadcasted_iota(jnp.int32, (LANES, nodes), 1)
    halo_iota = lax.broadcasted_iota(jnp.int32, (LANES, n * hcap), 1) + nodes
    node_iota = lax.broadcasted_iota(jnp.int32, (nodes, LANES), 0)
    for part in range(edge_count // LANES):
        rows = pl.ds(part * LANES, LANES)
        sender = sender_columns[:, part : part + 1]
        receiver = receiver_columns[:, part : part + 1]
        near_hot[rows, :nodes] = hot(sender == near_iota)
        near_hot[rows, nodes:] = hot(receiver == near_iota)
        halo_hot[rows, :] = hot(sender == halo_iota)
        node_hot[:, part * LANES : (part + 1) * LANES] = hot(
            receivers[part : part + 1, :] == node_iota
        )
    list_iota = lax.broadcasted_iota(jnp.int32, (hcap, nodes), 1)
    for p in range(n):
        list_hot[p * hcap : (p + 1) * hcap, :] = hot(list_columns[:, p : p + 1] == list_iota)

    gathered = collect(half, n)
    relay.wait_recv()
    gathered = gathered + relay_in[...].astype(F32)

    for i in (3, 10, 11, 12, 13):
        loads[i].wait()
    state = update(embed[...], gathered, w_enc_first, w_enc_second)
    sent = dot(state, w_send[...]).astype(BF16)
    halo_out[...] = dot(list_hot[...], sent).astype(BF16).reshape(n, hcap, width)
    halo_copies = []
    for t in range(n - 1):
        copy = pltpu.make_async_remote_copy(
            src_ref=halo_out.at[peer(t)],
            dst_ref=halo_in.at[me],
            send_sem=halo_send.at[t],
            recv_sem=halo_recv.at[t],
            device_id={"mesh": peer(t)},
            device_id_type=MESH,
        )
        copy.start()
        halo_copies.append(copy)
    halo_in[me] = halo_out[me]
    local_table[:nodes, :] = sent
    local_table[nodes:, :] = dot(state, w_recv[...]).astype(BF16)
    for chunk in range(edge_count // CHUNK):
        rows = pl.ds(chunk * CHUNK, CHUNK)
        pre[rows, :] += dot(near_hot[rows, :], local_table[...])

    for copy in halo_copies:
        copy.wait_recv()
    halo = halo_in[...].reshape(n * hcap, width)
    summed = jnp.zeros((nodes, width), F32)
    for chunk in range(edge_count // CHUNK):
        rows = pl.ds(chunk * CHUNK, CHUNK)
        edge_pre = pre[rows, :] + dot(halo_hot[rows, :], halo)
        summed = summed + dot(
            node_hot[:, chunk * CHUNK : (chunk + 1) * CHUNK], silu(edge_pre).astype(BF16)
        )
    for i in (15, 16, 17):
        loads[i].wait()
    node_sum = dot(summed.astype(BF16), w_message[...])
    out_ref[...] = update(state, node_sum, w_proc_first, w_proc_second)
    relay.wait_send()
    for id_copy, row_copy in copies.values():
        id_copy.wait_send()
        row_copy.wait_send()
    for copy in halo_copies:
        copy.wait_send()


def per_device(
    grid_in, owner, node_slot, mesh_embed, edge_latent, senders, receivers, send_list, *weights
):
    n = lax.axis_size("mesh")
    grid_count = grid_in.shape[0]
    nodes, width = mesh_embed.shape
    edge_count = edge_latent.shape[0]
    list_size = send_list.shape[1]
    cap = max(16, 2 * grid_count // n)
    hcap = max(16, list_size)
    if hcap != list_size:
        beyond = jnp.maximum(senders - nodes, 0)
        moved = nodes + beyond // list_size * hcap + beyond % list_size
        senders = jnp.where(senders < nodes, senders, moved)
        send_list = jnp.pad(send_list, ((0, 0), (0, hcap - list_size)))
    inputs = (
        grid_in.T,
        owner.reshape(1, grid_count),
        node_slot.reshape(1, grid_count),
        mesh_embed,
        edge_latent,
        senders.reshape(edge_count // LANES, LANES),
        receivers.reshape(edge_count // LANES, LANES),
        send_list,
    ) + weights
    dma = pltpu.SemaphoreType.DMA
    scratch = [pltpu.VMEM(x.shape, x.dtype) for x in inputs] + [
        pltpu.VMEM((grid_count, width), BF16),
        pltpu.VMEM((n, cap, width), BF16),
        pltpu.VMEM((n, cap, width), BF16),
        pltpu.VMEM((n, 1, GROUP), F32),
        pltpu.VMEM((n, 1, GROUP), F32),
        pltpu.VMEM((edge_count, width), F32),
        pltpu.VMEM((2 * nodes, width), BF16),
        pltpu.VMEM((edge_count, 2 * nodes), BF16),
        pltpu.VMEM((edge_count, n * hcap), BF16),
        pltpu.VMEM((nodes, edge_count), BF16),
        pltpu.VMEM((n * hcap, nodes), BF16),
        pltpu.VMEM((n, hcap, width), BF16),
        pltpu.VMEM((n, hcap, width), BF16),
        pltpu.VMEM((nodes, width), BF16),
        pltpu.VMEM((nodes, width), BF16),
        dma((2,)),
        dma((len(inputs),)),
        dma((n,)),
        dma((n,)),
        dma((n,)),
        dma((n,)),
        dma((n,)),
        dma((n,)),
    ]
    return pl.pallas_call(
        functools.partial(kernel, n, cap, hcap),
        out_shape=jax.ShapeDtypeStruct((nodes, width), BF16),
        in_specs=[pl.BlockSpec(memory_space=pl.ANY)] * len(inputs),
        out_specs=pl.BlockSpec(memory_space=pltpu.VMEM),
        scratch_shapes=scratch,
        compiler_params=pltpu.CompilerParams(
            collective_id=0, has_side_effects=True, vmem_limit_bytes=56 << 20
        ),
    )(*inputs)


def solution(mesh):
    rows, split, full = P(("groups", "mesh"), None), P("mesh"), P()
    in_specs = (rows, split, split, rows, rows, split, split, split) + (full,) * 10
    return jax.shard_map(
        per_device, mesh=mesh, in_specs=in_specs, out_specs=rows, check_vma=False
    )
```

```python
import functools

import jax
import jax.numpy as jnp
from jax import lax
from jax.experimental import pallas as pl
from jax.experimental.pallas import tpu as pltpu
from jax.sharding import PartitionSpec as P

F32 = jnp.float32
BF16 = jnp.bfloat16
MESH = pl.DeviceIdType.MESH
GROUP = 256
CHUNK = 256
LANES = 128


def dot(left, right):
    return jnp.dot(left, right, preferred_element_type=F32)


def silu(x):
    half = 0.5 * x
    return half * jnp.tanh(half) + half


def normalize(values):
    center = values - jnp.mean(values, -1, keepdims=True)
    spread = jnp.mean(center * center, -1, keepdims=True)
    return center * lax.rsqrt(spread + 1e-05)


def hot(flags):
    return jnp.where(flags, 1.0, 0.0).astype(BF16)


def update(state, gathered, w_first, w_second):
    width = state.shape[1]
    rows = state.astype(F32)
    mean = (
        jnp.sum(rows, -1, keepdims=True) + jnp.sum(gathered, -1, keepdims=True)
    ) / (2 * width)
    low, high = rows - mean, gathered - mean
    spread = (
        jnp.sum(low * low, -1, keepdims=True) + jnp.sum(high * high, -1, keepdims=True)
    ) / (2 * width)
    scale = lax.rsqrt(spread + 1e-05)
    hidden = dot((low * scale).astype(BF16), w_first[:width, :])
    hidden = hidden + dot((high * scale).astype(BF16), w_first[width:, :])
    return (rows + dot(silu(hidden).astype(BF16), w_second[...])).astype(BF16)


def kernel(n, cap, hcap, *refs):
    hbm = refs[:18]
    out_ref = refs[18]
    (
        grid_in,
        owner,
        node_slot,
        embed,
        edges,
        senders,
        receivers,
        send_list,
        w_grid_first,
        w_grid_second,
        w_enc_first,
        w_enc_second,
        w_send,
        w_recv,
        w_edge,
        w_message,
        w_proc_first,
        w_proc_second,
    ) = vmem = refs[19:37]
    (
        latent,
        outgoing,
        arrived,
        ids_out,
        ids_in,
        pre,
        local_table,
        near_hot,
        halo_hot,
        node_hot,
        list_hot,
        halo_out,
        halo_in,
        relay_out,
        relay_in,
        relay_sem,
        load_sem,
        row_send,
        row_recv,
        id_send,
        id_recv,
        halo_send,
        halo_recv,
    ) = refs[37:]
    grid_count = grid_in.shape[1]
    nodes, width = embed.shape
    edge_count = edges.shape[0]
    me = lax.axis_index("mesh")

    half = n // 2
    base = me // half * half
    mirror = lax.rem(me + half, n)

    def direct(place):
        return (1 - place % 2) * (1 - place % half // (half // 2))

    def around(t, count):
        return count // 2 - (t + 1) // 2 if t % 2 else count // 2 + t // 2

    def peer(t):
        return lax.rem(me + around(t, n), n)

    def near_peer(t):
        return base + lax.rem(me + around(t, half), half)

    loads = [
        pltpu.make_async_copy(source, target, load_sem.at[i])
        for i, (source, target) in enumerate(zip(hbm, vmem))
    ]
    for i in (0, 8, 1, 2, 9, 14, 4, 3, 10, 11, 7, 12, 13, 5, 6, 15, 16, 17):
        loads[i].start()
    barrier = pltpu.get_barrier_semaphore()
    for t in range(n - 1):
        pl.semaphore_signal(barrier, inc=1, device_id={"mesh": peer(t)}, device_id_type=MESH)

    loads[1].wait()
    loads[2].wait()
    block = lax.broadcasted_iota(jnp.int32, (n, 1), 0)
    step = lax.rem(block, half)
    turn = half // 2 + jnp.where(step % 2 == 1, -((step + 1) // 2), step // 2)
    target = base + lax.rem(me + turn, half)
    target = jnp.where(block < half, lax.rem(target + half, n), target)
    flags = jnp.where(target == owner[...], 1.0, 0.0)
    earlier = hot(
        lax.broadcasted_iota(jnp.int32, (grid_count, grid_count), 0)
        < lax.broadcasted_iota(jnp.int32, (grid_count, grid_count), 1)
    )
    rank = dot(flags.astype(BF16), earlier) + (block * cap).astype(F32)
    place = jnp.sum(flags * rank, 0, keepdims=True).astype(jnp.int32)
    slots = (flags * (node_slot[...] + 1).astype(F32)).astype(BF16)
    lane_hot = hot(
        lax.broadcasted_iota(jnp.int32, (GROUP, grid_count), 0) == place % GROUP
    )
    ids = lax.dot_general(slots, lane_hot, (((1,), (1,)), ((), ())), preferred_element_type=F32)
    for t in range(n):
        ids_out[t] = ids[t : t + 1, :]
    ids_in[n - 1] = ids[n - 1 : n, :]

    loads[0].wait()
    loads[8].wait()
    loads[9].wait()
    hidden = lax.dot_general(
        grid_in[...], w_grid_first[...], (((0,), (0,)), ((), ())), preferred_element_type=F32
    )
    hidden = silu(hidden).astype(BF16)
    latent[...] = normalize(dot(hidden, w_grid_second[...])).astype(BF16)

    pl.semaphore_wait(barrier, n - 1)
    per_group = GROUP // cap
    copies = {}
    for group in range(n // per_group):
        pack = hot(
            lax.broadcasted_iota(jnp.int32, (GROUP, grid_count), 0) + group * GROUP == place
        )
        packed = dot(pack, latent[...]).astype(BF16)
        first = group * per_group
        outgoing[first : first + per_group] = packed.reshape(per_group, cap, width)
        for t in range(first, first + per_group):
            if t == n - 1:
                arrived[t] = outgoing[t]
                continue
            receiver = near_peer(t % half)
            if t < half:
                receiver = lax.rem(receiver + half * direct(receiver), n)
            id_copy = pltpu.make_async_remote_copy(
                src_ref=ids_out.at[t],
                dst_ref=ids_in.at[t],
                send_sem=id_send.at[t],
                recv_sem=id_recv.at[t],
                device_id={"mesh": mirror if t == half - 1 else receiver},
                device_id_type=MESH,
            )
            row_copy = pltpu.make_async_remote_copy(
                src_ref=outgoing.at[t],
                dst_ref=arrived.at[t],
                send_sem=row_send.at[t],
                recv_sem=row_recv.at[t],
                device_id={"mesh": mirror if t == half - 1 else receiver},
                device_id_type=MESH,
            )
            copies[t] = (id_copy, row_copy)
            if t == half - 1:

                @pl.when(direct(me) == 1)
                def _():
                    copies[half - 1][0].start()
                    copies[half - 1][1].start()

                @pl.when(direct(me) == 0)
                def _():
                    ids_in[half - 1] = ids_out[half - 1]
                    arrived[half - 1] = outgoing[half - 1]
            else:
                id_copy.start()
                row_copy.start()

    loads[14].wait()
    loads[4].wait()
    for chunk in range(edge_count // CHUNK):
        rows = pl.ds(chunk * CHUNK, CHUNK)
        pre[rows, :] = dot(edges[rows, :], w_edge[...])

    slot_iota = lax.broadcasted_iota(jnp.int32, (nodes, GROUP), 0).astype(F32) + 1.0

    def collect(start, stop):
        total = jnp.zeros((nodes, width), F32)
        for first in range(start, stop, per_group):
            named = jnp.zeros((1, GROUP), F32)
            for t in range(first, first + per_group):
                if t == half - 1:

                    @pl.when(direct(me) == 1)
                    def _():
                        copies[half - 1][0].wait_recv()
                        copies[half - 1][1].wait_recv()
                elif t in copies:
                    copies[t][0].wait_recv()
                    copies[t][1].wait_recv()
                named = named + ids_in[t]
            total = total + dot(
                hot(slot_iota == named),
                arrived[first : first + per_group].reshape(GROUP, width),
            )
        return total

    relay_out[...] = collect(0, half).astype(BF16)
    relay = pltpu.make_async_remote_copy(
        src_ref=relay_out,
        dst_ref=relay_in,
        send_sem=relay_sem.at[0],
        recv_sem=relay_sem.at[1],
        device_id={"mesh": mirror},
        device_id_type=MESH,
    )

    @pl.when(direct(me) == 0)
    def _():
        relay.start()

    @pl.when(direct(me) == 1)
    def _():
        relay_in[...] = relay_out[...]

    loads[5].wait()
    loads[6].wait()
    loads[7].wait()
    sender_columns = jnp.transpose(senders[...])
    receiver_columns = jnp.transpose(receivers[...])
    list_columns = jnp.transpose(send_list[...])
    near_iota = lax.broadcasted_iota(jnp.int32, (LANES, nodes), 1)
    halo_iota = lax.broadcasted_iota(jnp.int32, (LANES, n * hcap), 1) + nodes
    node_iota = lax.broadcasted_iota(jnp.int32, (nodes, LANES), 0)
    for part in range(edge_count // LANES):
        rows = pl.ds(part * LANES, LANES)
        sender = sender_columns[:, part : part + 1]
        receiver = receiver_columns[:, part : part + 1]
        near_hot[rows, :nodes] = hot(sender == near_iota)
        near_hot[rows, nodes:] = hot(receiver == near_iota)
        halo_hot[rows, :] = hot(sender == halo_iota)
        node_hot[:, part * LANES : (part + 1) * LANES] = hot(
            receivers[part : part + 1, :] == node_iota
        )
    list_iota = lax.broadcasted_iota(jnp.int32, (hcap, nodes), 1)
    for p in range(n):
        list_hot[p * hcap : (p + 1) * hcap, :] = hot(list_columns[:, p : p + 1] == list_iota)

    gathered = collect(half, n)

    @pl.when(direct(me) == 0)
    def _():
        relay.wait_recv()

    gathered = gathered + relay_in[...].astype(F32)

    for i in (3, 10, 11, 12, 13):
        loads[i].wait()
    state = update(embed[...], gathered, w_enc_first, w_enc_second)
    sent = dot(state, w_send[...]).astype(BF16)
    halo_out[...] = dot(list_hot[...], sent).astype(BF16).reshape(n, hcap, width)
    halo_copies = []
    for t in range(n - 1):
        copy = pltpu.make_async_remote_copy(
            src_ref=halo_out.at[peer(t)],
            dst_ref=halo_in.at[me],
            send_sem=halo_send.at[t],
            recv_sem=halo_recv.at[t],
            device_id={"mesh": peer(t)},
            device_id_type=MESH,
        )
        copy.start()
        halo_copies.append(copy)
    halo_in[me] = halo_out[me]
    local_table[:nodes, :] = sent
    local_table[nodes:, :] = dot(state, w_recv[...]).astype(BF16)
    for chunk in range(edge_count // CHUNK):
        rows = pl.ds(chunk * CHUNK, CHUNK)
        pre[rows, :] += dot(near_hot[rows, :], local_table[...])

    for copy in halo_copies:
        copy.wait_recv()
    halo = halo_in[...].reshape(n * hcap, width)
    summed = jnp.zeros((nodes, width), F32)
    for chunk in range(edge_count // CHUNK):
        rows = pl.ds(chunk * CHUNK, CHUNK)
        edge_pre = pre[rows, :] + dot(halo_hot[rows, :], halo)
        summed = summed + dot(
            node_hot[:, chunk * CHUNK : (chunk + 1) * CHUNK], silu(edge_pre).astype(BF16)
        )
    for i in (15, 16, 17):
        loads[i].wait()
    node_sum = dot(summed.astype(BF16), w_message[...])
    out_ref[...] = update(state, node_sum, w_proc_first, w_proc_second)

    @pl.when(direct(me) == 0)
    def _():
        relay.wait_send()

    @pl.when(direct(me) == 1)
    def _():
        copies[half - 1][0].wait_send()
        copies[half - 1][1].wait_send()

    for t, (id_copy, row_copy) in copies.items():
        if t != half - 1:
            id_copy.wait_send()
            row_copy.wait_send()
    for copy in halo_copies:
        copy.wait_send()


def per_device(
    grid_in, owner, node_slot, mesh_embed, edge_latent, senders, receivers, send_list, *weights
):
    n = lax.axis_size("mesh")
    grid_count = grid_in.shape[0]
    nodes, width = mesh_embed.shape
    edge_count = edge_latent.shape[0]
    list_size = send_list.shape[1]
    cap = max(16, 2 * grid_count // n)
    hcap = max(16, list_size)
    if hcap != list_size:
        beyond = jnp.maximum(senders - nodes, 0)
        moved = nodes + beyond // list_size * hcap + beyond % list_size
        senders = jnp.where(senders < nodes, senders, moved)
        send_list = jnp.pad(send_list, ((0, 0), (0, hcap - list_size)))
    inputs = (
        grid_in.T,
        owner.reshape(1, grid_count),
        node_slot.reshape(1, grid_count),
        mesh_embed,
        edge_latent,
        senders.reshape(edge_count // LANES, LANES),
        receivers.reshape(edge_count // LANES, LANES),
        send_list,
    ) + weights
    dma = pltpu.SemaphoreType.DMA
    scratch = [pltpu.VMEM(x.shape, x.dtype) for x in inputs] + [
        pltpu.VMEM((grid_count, width), BF16),
        pltpu.VMEM((n, cap, width), BF16),
        pltpu.VMEM((n, cap, width), BF16),
        pltpu.VMEM((n, 1, GROUP), F32),
        pltpu.VMEM((n, 1, GROUP), F32),
        pltpu.VMEM((edge_count, width), F32),
        pltpu.VMEM((2 * nodes, width), BF16),
        pltpu.VMEM((edge_count, 2 * nodes), BF16),
        pltpu.VMEM((edge_count, n * hcap), BF16),
        pltpu.VMEM((nodes, edge_count), BF16),
        pltpu.VMEM((n * hcap, nodes), BF16),
        pltpu.VMEM((n, hcap, width), BF16),
        pltpu.VMEM((n, hcap, width), BF16),
        pltpu.VMEM((nodes, width), BF16),
        pltpu.VMEM((nodes, width), BF16),
        dma((2,)),
        dma((len(inputs),)),
        dma((n,)),
        dma((n,)),
        dma((n,)),
        dma((n,)),
        dma((n,)),
        dma((n,)),
    ]
    return pl.pallas_call(
        functools.partial(kernel, n, cap, hcap),
        out_shape=jax.ShapeDtypeStruct((nodes, width), BF16),
        in_specs=[pl.BlockSpec(memory_space=pl.ANY)] * len(inputs),
        out_specs=pl.BlockSpec(memory_space=pltpu.VMEM),
        scratch_shapes=scratch,
        compiler_params=pltpu.CompilerParams(
            collective_id=0, has_side_effects=True, vmem_limit_bytes=56 << 20
        ),
    )(*inputs)


def solution(mesh):
    rows, split, full = P(("groups", "mesh"), None), P("mesh"), P()
    in_specs = (rows, split, split, rows, rows, split, split, split) + (full,) * 10
    return jax.shard_map(
        per_device, mesh=mesh, in_specs=in_specs, out_specs=rows, check_vma=False
    )
```

```python
import functools

import jax
import jax.numpy as jnp
from jax import lax
from jax.experimental import pallas as pl
from jax.experimental.pallas import tpu as pltpu
from jax.sharding import PartitionSpec as P

F32 = jnp.float32
BF16 = jnp.bfloat16
MESH = pl.DeviceIdType.MESH
GROUP = 256
CHUNK = 256
LANES = 128


def dot(left, right):
    return jnp.dot(left, right, preferred_element_type=F32)


def silu(x):
    half = 0.5 * x
    return half * jnp.tanh(half) + half


def normalize(values):
    center = values - jnp.mean(values, -1, keepdims=True)
    spread = jnp.mean(center * center, -1, keepdims=True)
    return center * lax.rsqrt(spread + 1e-05)


def hot(flags):
    return jnp.where(flags, 1.0, 0.0).astype(BF16)


def update(state, gathered, w_first, w_second):
    width = state.shape[1]
    rows = state.astype(F32)
    mean = (
        jnp.sum(rows, -1, keepdims=True) + jnp.sum(gathered, -1, keepdims=True)
    ) / (2 * width)
    low, high = rows - mean, gathered - mean
    spread = (
        jnp.sum(low * low, -1, keepdims=True) + jnp.sum(high * high, -1, keepdims=True)
    ) / (2 * width)
    scale = lax.rsqrt(spread + 1e-05)
    hidden = dot((low * scale).astype(BF16), w_first[:width, :])
    hidden = hidden + dot((high * scale).astype(BF16), w_first[width:, :])
    return (rows + dot(silu(hidden).astype(BF16), w_second[...])).astype(BF16)


def kernel(n, cap, hcap, *refs):
    hbm = refs[:18]
    out_ref = refs[18]
    (
        grid_in,
        owner,
        node_slot,
        embed,
        edges,
        senders,
        receivers,
        send_list,
        w_grid_first,
        w_grid_second,
        w_enc_first,
        w_enc_second,
        w_send,
        w_recv,
        w_edge,
        w_message,
        w_proc_first,
        w_proc_second,
    ) = vmem = refs[19:37]
    (
        latent,
        outgoing,
        arrived,
        ids_out,
        ids_in,
        pre,
        local_table,
        near_hot,
        halo_hot,
        node_hot,
        list_hot,
        halo_out,
        halo_in,
        relay_out,
        relay_in,
        relay_sem,
        load_sem,
        row_send,
        row_recv,
        id_send,
        id_recv,
        halo_send,
        halo_recv,
    ) = refs[37:]
    grid_count = grid_in.shape[1]
    nodes, width = embed.shape
    edge_count = edges.shape[0]
    me = lax.axis_index("mesh")

    half = n // 2
    base = me // half * half
    mirror = lax.rem(me + half, n)

    def direct(place):
        return (1 - place % 2) * (1 - place % half // (half // 2))

    def around(t, count):
        return count // 2 - (t + 1) // 2 if t % 2 else count // 2 + t // 2

    def peer(t):
        return lax.rem(me + around(t, n), n)

    def near_peer(t):
        return base + lax.rem(me + around(t, half), half)

    loads = [
        pltpu.make_async_copy(source, target, load_sem.at[i])
        for i, (source, target) in enumerate(zip(hbm, vmem))
    ]
    for i in (0, 8, 1, 2, 9, 14, 4, 3, 10, 11, 7, 12, 13, 5, 6, 15, 16, 17):
        loads[i].start()
    barrier = pltpu.get_barrier_semaphore()
    for t in range(n - 1):
        pl.semaphore_signal(barrier, inc=1, device_id={"mesh": peer(t)}, device_id_type=MESH)

    loads[1].wait()
    loads[2].wait()
    block = lax.broadcasted_iota(jnp.int32, (n, 1), 0)
    step = lax.rem(block, half)
    turn = half // 2 + jnp.where(step % 2 == 1, -((step + 1) // 2), step // 2)
    target = base + lax.rem(me + turn, half)
    target = jnp.where(block < half, lax.rem(target + half, n), target)
    flags = jnp.where(target == owner[...], 1.0, 0.0)
    earlier = hot(
        lax.broadcasted_iota(jnp.int32, (grid_count, grid_count), 0)
        < lax.broadcasted_iota(jnp.int32, (grid_count, grid_count), 1)
    )
    rank = dot(flags.astype(BF16), earlier) + (block * cap).astype(F32)
    place = jnp.sum(flags * rank, 0, keepdims=True).astype(jnp.int32)
    slots = (flags * (node_slot[...] + 1).astype(F32)).astype(BF16)
    lane_hot = hot(
        lax.broadcasted_iota(jnp.int32, (GROUP, grid_count), 0) == place % GROUP
    )
    ids = lax.dot_general(slots, lane_hot, (((1,), (1,)), ((), ())), preferred_element_type=F32)
    for t in range(n):
        ids_out[t] = ids[t : t + 1, :]
    ids_in[n - 1] = ids[n - 1 : n, :]

    loads[0].wait()
    loads[8].wait()
    loads[9].wait()
    hidden = lax.dot_general(
        grid_in[...], w_grid_first[...], (((0,), (0,)), ((), ())), preferred_element_type=F32
    )
    hidden = silu(hidden).astype(BF16)
    latent[...] = normalize(dot(hidden, w_grid_second[...])).astype(BF16)

    pl.semaphore_wait(barrier, n - 1)
    per_group = GROUP // cap
    copies = {}
    for group in range(n // per_group):
        pack = hot(
            lax.broadcasted_iota(jnp.int32, (GROUP, grid_count), 0) + group * GROUP == place
        )
        packed = dot(pack, latent[...]).astype(BF16)
        first = group * per_group
        outgoing[first : first + per_group] = packed.reshape(per_group, cap, width)
        for t in range(first, first + per_group):
            if t == n - 1:
                arrived[t] = outgoing[t]
                continue
            receiver = near_peer(t % half)
            if t < half:
                receiver = lax.rem(receiver + half * direct(receiver), n)
            id_copy = pltpu.make_async_remote_copy(
                src_ref=ids_out.at[t],
                dst_ref=ids_in.at[t],
                send_sem=id_send.at[t],
                recv_sem=id_recv.at[t],
                device_id={"mesh": mirror if t == half - 1 else receiver},
                device_id_type=MESH,
            )
            row_copy = pltpu.make_async_remote_copy(
                src_ref=outgoing.at[t],
                dst_ref=arrived.at[t],
                send_sem=row_send.at[t],
                recv_sem=row_recv.at[t],
                device_id={"mesh": mirror if t == half - 1 else receiver},
                device_id_type=MESH,
            )
            copies[t] = (id_copy, row_copy)
            if t == half - 1:

                @pl.when(direct(me) == 1)
                def _():
                    copies[half - 1][0].start()
                    copies[half - 1][1].start()

                @pl.when(direct(me) == 0)
                def _():
                    ids_in[half - 1] = ids_out[half - 1]
                    arrived[half - 1] = outgoing[half - 1]
            else:
                id_copy.start()
                row_copy.start()

    loads[14].wait()
    loads[4].wait()
    for chunk in range(edge_count // CHUNK):
        rows = pl.ds(chunk * CHUNK, CHUNK)
        pre[rows, :] = dot(edges[rows, :], w_edge[...])

    slot_iota = lax.broadcasted_iota(jnp.int32, (nodes, GROUP), 0).astype(F32) + 1.0

    def collect(start, stop):
        total = jnp.zeros((nodes, width), F32)
        for first in range(start, stop, per_group):
            named = jnp.zeros((1, GROUP), F32)
            for t in range(first, first + per_group):
                if t == half - 1:

                    @pl.when(direct(me) == 1)
                    def _():
                        copies[half - 1][0].wait_recv()
                        copies[half - 1][1].wait_recv()
                elif t in copies:
                    copies[t][0].wait_recv()
                    copies[t][1].wait_recv()
                named = named + ids_in[t]
            total = total + dot(
                hot(slot_iota == named),
                arrived[first : first + per_group].reshape(GROUP, width),
            )
        return total

    relay_out[...] = collect(0, half).astype(BF16)
    relay = pltpu.make_async_remote_copy(
        src_ref=relay_out,
        dst_ref=relay_in,
        send_sem=relay_sem.at[0],
        recv_sem=relay_sem.at[1],
        device_id={"mesh": mirror},
        device_id_type=MESH,
    )

    @pl.when(direct(me) == 0)
    def _():
        relay.start()

    @pl.when(direct(me) == 1)
    def _():
        relay_in[...] = relay_out[...]

    loads[5].wait()
    loads[6].wait()
    loads[7].wait()
    sender_columns = jnp.transpose(senders[...])
    receiver_columns = jnp.transpose(receivers[...])
    list_columns = jnp.transpose(send_list[...])
    near_iota = lax.broadcasted_iota(jnp.int32, (LANES, nodes), 1)
    lane = lax.broadcasted_iota(jnp.int32, (1, n * hcap), 1)
    slot = lane // hcap
    near = slot // half
    back = slot % half
    back = half // 2 + jnp.where(back % 2 == 1, -((back + 1) // 2), back // 2)
    source = base + lax.rem(me + n - back, half)
    source = jnp.where(near == 1, source, lax.rem(source + half, n))
    halo_place = nodes + source * hcap + lane % hcap
    node_iota = lax.broadcasted_iota(jnp.int32, (nodes, LANES), 0)
    for part in range(edge_count // LANES):
        rows = pl.ds(part * LANES, LANES)
        sender = sender_columns[:, part : part + 1]
        receiver = receiver_columns[:, part : part + 1]
        near_hot[rows, :nodes] = hot(sender == near_iota)
        near_hot[rows, nodes:] = hot(receiver == near_iota)
        halo_hot[rows, :] = hot(sender == halo_place)
        node_hot[:, part * LANES : (part + 1) * LANES] = hot(
            receivers[part : part + 1, :] == node_iota
        )
    list_iota = lax.broadcasted_iota(jnp.int32, (hcap, nodes), 1)
    for p in range(n):
        list_hot[p * hcap : (p + 1) * hcap, :] = hot(list_columns[:, p : p + 1] == list_iota)

    gathered = collect(half, n)

    @pl.when(direct(me) == 0)
    def _():
        relay.wait_recv()

    gathered = gathered + relay_in[...].astype(F32)

    for i in (3, 10, 11, 12, 13):
        loads[i].wait()
    state = update(embed[...], gathered, w_enc_first, w_enc_second)
    sent = dot(state, w_send[...]).astype(BF16)
    halo_out[...] = dot(list_hot[...], sent).astype(BF16).reshape(n, hcap, width)
    halo_copies = {}
    for t in range(half):
        for far in (1, 0):
            slot = t if far else half + t
            if slot == n - 1:
                continue
            receiver = lax.rem(near_peer(t) + half * far, n)
            halo_copies[slot] = pltpu.make_async_remote_copy(
                src_ref=halo_out.at[receiver],
                dst_ref=halo_in.at[slot],
                send_sem=halo_send.at[slot],
                recv_sem=halo_recv.at[slot],
                device_id={"mesh": receiver},
                device_id_type=MESH,
            )
            halo_copies[slot].start()
    halo_in[n - 1] = halo_out[me]
    local_table[:nodes, :] = sent
    local_table[nodes:, :] = dot(state, w_recv[...]).astype(BF16)
    for chunk in range(edge_count // CHUNK):
        rows = pl.ds(chunk * CHUNK, CHUNK)
        pre[rows, :] += dot(near_hot[rows, :], local_table[...])

    for slot in range(half, n - 1):
        halo_copies[slot].wait_recv()
    inner = half * hcap
    halo = halo_in[half:].reshape(inner, width)
    for chunk in range(edge_count // CHUNK):
        rows = pl.ds(chunk * CHUNK, CHUNK)
        pre[rows, :] += dot(halo_hot[rows, inner:], halo)
    for slot in range(half):
        halo_copies[slot].wait_recv()
    halo = halo_in[:half].reshape(inner, width)
    summed = jnp.zeros((nodes, width), F32)
    for chunk in range(edge_count // CHUNK):
        rows = pl.ds(chunk * CHUNK, CHUNK)
        edge_pre = pre[rows, :] + dot(halo_hot[rows, :inner], halo)
        summed = summed + dot(
            node_hot[:, chunk * CHUNK : (chunk + 1) * CHUNK], silu(edge_pre).astype(BF16)
        )
    for i in (15, 16, 17):
        loads[i].wait()
    node_sum = dot(summed.astype(BF16), w_message[...])
    out_ref[...] = update(state, node_sum, w_proc_first, w_proc_second)

    @pl.when(direct(me) == 0)
    def _():
        relay.wait_send()

    @pl.when(direct(me) == 1)
    def _():
        copies[half - 1][0].wait_send()
        copies[half - 1][1].wait_send()

    for t, (id_copy, row_copy) in copies.items():
        if t != half - 1:
            id_copy.wait_send()
            row_copy.wait_send()
    for copy in halo_copies.values():
        copy.wait_send()


def per_device(
    grid_in, owner, node_slot, mesh_embed, edge_latent, senders, receivers, send_list, *weights
):
    n = lax.axis_size("mesh")
    grid_count = grid_in.shape[0]
    nodes, width = mesh_embed.shape
    edge_count = edge_latent.shape[0]
    list_size = send_list.shape[1]
    cap = max(16, 2 * grid_count // n)
    hcap = max(16, list_size)
    if hcap != list_size:
        beyond = jnp.maximum(senders - nodes, 0)
        moved = nodes + beyond // list_size * hcap + beyond % list_size
        senders = jnp.where(senders < nodes, senders, moved)
        send_list = jnp.pad(send_list, ((0, 0), (0, hcap - list_size)))
    inputs = (
        grid_in.T,
        owner.reshape(1, grid_count),
        node_slot.reshape(1, grid_count),
        mesh_embed,
        edge_latent,
        senders.reshape(edge_count // LANES, LANES),
        receivers.reshape(edge_count // LANES, LANES),
        send_list,
    ) + weights
    dma = pltpu.SemaphoreType.DMA
    scratch = [pltpu.VMEM(x.shape, x.dtype) for x in inputs] + [
        pltpu.VMEM((grid_count, width), BF16),
        pltpu.VMEM((n, cap, width), BF16),
        pltpu.VMEM((n, cap, width), BF16),
        pltpu.VMEM((n, 1, GROUP), F32),
        pltpu.VMEM((n, 1, GROUP), F32),
        pltpu.VMEM((edge_count, width), F32),
        pltpu.VMEM((2 * nodes, width), BF16),
        pltpu.VMEM((edge_count, 2 * nodes), BF16),
        pltpu.VMEM((edge_count, n * hcap), BF16),
        pltpu.VMEM((nodes, edge_count), BF16),
        pltpu.VMEM((n * hcap, nodes), BF16),
        pltpu.VMEM((n, hcap, width), BF16),
        pltpu.VMEM((n, hcap, width), BF16),
        pltpu.VMEM((nodes, width), BF16),
        pltpu.VMEM((nodes, width), BF16),
        dma((2,)),
        dma((len(inputs),)),
        dma((n,)),
        dma((n,)),
        dma((n,)),
        dma((n,)),
        dma((n,)),
        dma((n,)),
    ]
    return pl.pallas_call(
        functools.partial(kernel, n, cap, hcap),
        out_shape=jax.ShapeDtypeStruct((nodes, width), BF16),
        in_specs=[pl.BlockSpec(memory_space=pl.ANY)] * len(inputs),
        out_specs=pl.BlockSpec(memory_space=pltpu.VMEM),
        scratch_shapes=scratch,
        compiler_params=pltpu.CompilerParams(
            collective_id=0, has_side_effects=True, vmem_limit_bytes=56 << 20
        ),
    )(*inputs)


def solution(mesh):
    rows, split, full = P(("groups", "mesh"), None), P("mesh"), P()
    in_specs = (rows, split, split, rows, rows, split, split, split) + (full,) * 10
    return jax.shard_map(
        per_device, mesh=mesh, in_specs=in_specs, out_specs=rows, check_vma=False
    )
```
